512 devices in a mesh: space: 64 (over x, z), node: 4 (over y_hi, core), tm: 2 (over y_lo).
Axes of the slice: x: 4, y: 4 (y_hi: 2, y_lo: 2; y = y_hi * 2 + y_lo), z: 16, core: 2. Of those that a mesh axis runs over, the one named last changes fastest.
Arguments:
- start_old: float32 [2, 512, 128, 256], P('tm', 'space'), may hold values from -4 to 4
- nodes_old: float32 [2, 4, 512, 128, 256], P('tm', 'node', 'space'), may hold values from -4 to 4
Outputs:
- nodes_new: float32 [2, 4, 512, 128, 256], P('tm', 'node', 'space')
- end_new: float32 [2, 512, 128, 256], P('tm', 'space')
The draws below stay inside these ranges and needn't reach their ends.
All inputs are finite; a program needn't handle non-finite values.
Results may differ from the reference program's by a relative error of at most 0.00002.
Values sent between devices are 32-bit elements; how exact they have to be, the bound alone decides.
A program may use at most 64 MiB of HBM per device.

```python
import jax
import jax.numpy as jnp

NX = 256
NY = 128
NODES = 4
PASSES = 4
SLICES = 2
NZ = 512


def levels(key, dims, cuts, low, top_value):
    loudness, own = 1.0, jax.random.fold_in(key, 6)
    for axis_at, shards_of in cuts:
        draws = jnp.exp(jax.random.uniform(jax.random.fold_in(own, axis_at), (shards_of,), jnp.float32, low / len(cuts), top_value / len(cuts)))
        loudness = loudness * jnp.repeat(draws, dims[axis_at] // shards_of).reshape([-1 if axis == axis_at else 1 for axis in range(len(dims))])
    return loudness


def centred(own_key, dims, deviation, limit, split=(), dtype=jnp.bfloat16):
    entries = deviation * jax.random.normal(own_key, dims, jnp.float32)
    if split:
        entries = entries * levels(own_key, dims, split, -0.22, 0.18)
    return jnp.clip(entries, -limit, limit).astype(dtype)


def setup_inputs(seed: int = 0) -> dict:
    key_list = jax.random.split(jax.random.key(seed), 3)
    return {
        "start_old": centred(key_list[0], (SLICES, NZ, NY, NX), 1.0, 4.0, ((0, 2), (1, 64)), jnp.float32),
        "nodes_old": centred(key_list[1], (SLICES, NODES, NZ, NY, NX), 1.0, 4.0, ((0, 2), (1, 4), (2, 64)), jnp.float32),
    }


time_step = 0.25
diffusion = 4.0
reaction = 1.0


def collocation(count):
    points = [-0.8611363115940526, -0.3399810435848563, 0.3399810435848563, 0.8611363115940526]
    raw_weights = [0.3478548451374538, 0.6521451548625461, 0.6521451548625461, 0.3478548451374538]
    node_times = [(point + 1.0) / 2.0 for point in points]
    quadrature = [[0.0 for column in range(count)] for target in range(count)]
    for source in range(count):
        coeffs = [1.0]
        scaling = 1.0
        for other in range(count):
            if other != source:
                other_time = node_times[other]
                shifted = [0.0] + coeffs
                for power in range(len(coeffs)):
                    shifted[power] = shifted[power] - other_time * coeffs[power]
                coeffs = shifted
                scaling = scaling * (node_times[source] - other_time)
        for target in range(count):
            target_time = node_times[target]
            integral = 0.0
            for power in range(len(coeffs)):
                integral = integral + coeffs[power] * target_time ** (power + 1) / (power + 1)
            quadrature[target][source] = integral / scaling
    return node_times, quadrature, [weight / 2.0 for weight in raw_weights]


def neighbour_sum(values):
    total = jnp.roll(values, -1, 0) + jnp.roll(values, 1, 0)
    total = total + jnp.roll(values, -1, 1) + jnp.roll(values, 1, 1)
    total = total + jnp.roll(values, -1, 2) + jnp.roll(values, 1, 2)
    return total


def forcing(values):
    laplace = neighbour_sum(values) - 6.0 * values
    return laplace, diffusion * laplace + reaction * (values - values * values * values)


def reference(start_old, nodes_old):
    node_times, quadrature, weights = collocation(NODES)
    all_nodes = []
    all_ends = []
    previous_end = start_old[0]
    for interval in range(SLICES):
        laplaces = []
        forces = []
        for source in range(NODES):
            laplace, force = forcing(nodes_old[interval, source])
            laplaces.append(laplace)
            forces.append(force)
        weighted = jnp.zeros_like(forces[0])
        for source in range(NODES):
            weighted = weighted + float(weights[source]) * forces[source]
        end_old = start_old[interval] + time_step * weighted
        begin_state = start_old[0] if interval == 0 else previous_end
        previous_end = end_old
        new_nodes = []
        for target in range(NODES):
            quad_sum = jnp.zeros_like(forces[0])
            for source in range(NODES):
                quad_sum = quad_sum + float(quadrature[target][source]) * forces[source]
            implicit = time_step * diffusion * float(node_times[target])
            right_side = begin_state + time_step * quad_sum - implicit * laplaces[target]
            iterate = nodes_old[interval, target]
            for step_index in range(PASSES):
                iterate = (right_side + implicit * neighbour_sum(iterate)) / (1.0 + 6.0 * implicit)
            new_nodes.append(iterate)
        weighted_new = jnp.zeros_like(forces[0])
        for source in range(NODES):
            weighted_new = weighted_new + float(weights[source]) * forcing(new_nodes[source])[1]
        all_ends.append(begin_state + time_step * weighted_new)
        all_nodes.append(jnp.stack(new_nodes))
    return jnp.stack(all_nodes), jnp.stack(all_ends)
```

```python
import jax
import jax.numpy as jnp
from jax import lax
from jax.experimental import pallas as pl
from jax.experimental.pallas import tpu as pltpu
from jax.sharding import PartitionSpec as P

NODES = 4
time_step = 0.25
diffusion = 4.0
reaction = 1.0
MESH = pl.DeviceIdType.MESH
H = 4
NMSG = 80


def collocation(count):
    points = [-0.8611363115940526, -0.3399810435848563, 0.3399810435848563, 0.8611363115940526]
    raw_weights = [0.3478548451374538, 0.6521451548625461, 0.6521451548625461, 0.3478548451374538]
    node_times = [(point + 1.0) / 2.0 for point in points]
    quadrature = [[0.0 for column in range(count)] for target in range(count)]
    for source in range(count):
        coeffs = [1.0]
        scaling = 1.0
        for other in range(count):
            if other != source:
                other_time = node_times[other]
                shifted = [0.0] + coeffs
                for power in range(len(coeffs)):
                    shifted[power] = shifted[power] - other_time * coeffs[power]
                coeffs = shifted
                scaling = scaling * (node_times[source] - other_time)
        for target in range(count):
            target_time = node_times[target]
            integral = 0.0
            for power in range(len(coeffs)):
                integral = integral + coeffs[power] * target_time ** (power + 1) / (power + 1)
            quadrature[target][source] = integral / scaling
    return (node_times, quadrature, [weight / 2.0 for weight in raw_weights])


TIMES, QUAD, WEIGHTS = collocation(NODES)
IMPLICIT = [time_step * diffusion * t for t in TIMES]
SCALE = [1.0 / (1.0 + 6.0 * a) for a in IMPLICIT]
BETA = [a / (1.0 + 6.0 * a) for a in IMPLICIT]
LINEAR = reaction - 6.0 * diffusion


def pick(table, index):
    value = jnp.float32(table[-1])
    for at in range(len(table) - 2, -1, -1):
        value = jnp.where(index == at, jnp.float32(table[at]), value)
    return value


def flat_ring(x):
    return (pltpu.roll(x, 1, 0) + pltpu.roll(x, x.shape[0] - 1, 0)) + (
        pltpu.roll(x, 1, 1) + pltpu.roll(x, x.shape[1] - 1, 1)
    )


def kernel(spaces, start_ref, x_ref, new_ref, end_ref,
           XB, UB, RB, BG, DA, DB, EO, UX, VB, VR, send, recv, local):
    sp, nd, tm = lax.axis_index("space"), lax.axis_index("node"), lax.axis_index("tm")
    h, c = nd // 2, nd % 2
    zp, zm = (sp + 1) % spaces, (sp + spaces - 1) % spaces
    y = 2 * h + tm

    def at_y(by):
        to = (y + by) % 4
        return (sp, (to // 2) * 2 + c, to % 2)

    SIB = (sp, 2 * h + 1 - c, tm)
    PAR = (sp, 2 * (1 - h) + c, tm)
    ZP, ZM = (zp, nd, tm), (zm, nd, tm)
    YP, YM = at_y(1), at_y(3)

    barrier = pltpu.get_barrier_semaphore()
    for device in (SIB, PAR, ZP, ZM, YP, YM):
        pl.semaphore_signal(barrier, inc=1, device_id=device, device_id_type=MESH)

    own = x_ref.at[0, 0]
    begin_in = start_ref.at[0]
    loads = [pltpu.make_async_copy(own, XB.at[0, pl.ds(H, 8)], local.at[0])]
    loads[0].start()
    begin_load = pltpu.make_async_copy(begin_in, BG.at[pl.ds(3, 8)], local.at[1])

    @pl.when(tm == 0)
    def _():
        begin_load.start()

    pl.semaphore_wait(barrier, 6)

    count = [0]

    def message(src, dst, device):
        at = count[0]
        count[0] += 1
        return pltpu.make_async_remote_copy(
            src_ref=src, dst_ref=dst, send_sem=send.at[at], recv_sem=recv.at[at],
            device_id=device, device_id_type=MESH)

    order = [0, 7, 1, 6, 2, 5, 3, 4]
    f1 = {p: message(own.at[p], XB.at[2, H + p], PAR) for p in order}
    f2 = message(own, XB.at[1, pl.ds(H, 8)], SIB)
    f3 = {p: message(own.at[p], XB.at[0, H + 8 + p if p < 4 else p - 4], ZM if p < 4 else ZP) for p in order}
    for p in order[:2]:
        f1[p].start()
    f2.start()
    for p in order[:2]:
        f3[p].start()
    for p in order[2:]:
        f1[p].start()
        f3[p].start()
    b0 = message(begin_in.at[pl.ds(c * 5, 3)], BG.at[pl.ds((1 - c) * 11, 3)],
                 (jnp.where(c == 0, zm, zp), nd, tm))

    @pl.when(tm == 0)
    def _():
        b0.start()

    across = {p: message(XB.at[2, H + p], XB.at[3, H + p], SIB) for p in order}
    along = {p: message(XB.at[2, H + p], XB.at[2, H + 8 + p if p < 4 else p - 4], ZM if p < 4 else ZP) for p in order}
    rim = lambda p: H + 8 + p if p < 4 else p - 4
    own_rim = {p: message(XB.at[0, rim(p)], XB.at[1, rim(p)], SIB) for p in order}
    far_rim = {p: message(XB.at[2, rim(p)], XB.at[3, rim(p)], SIB) for p in order}
    hs = (1 - c) * 11
    b1 = message(BG.at[pl.ds(hs, 3)], BG.at[pl.ds(hs, 3)], SIB)
    eo, eb = [], []
    for k in range(4):
        p = k + c * (7 - 2 * k)
        rows = pl.ds(h * 64, 64)
        eo.append([message(EO.at[k, rows], BG.at[p + 3, rows], d) for d in (YP, YM)])
        entry = [message(BG.at[p + 3], BG.at[p + 3], SIB)]
        if k < 3:
            entry.append(message(BG.at[p + 3], BG.at[(1 - c) * (11 + k) + c * (2 - k)],
                                 (jnp.where(c == 0, zm, zp), nd, tm)))
        eb.append(entry)

    nodes = [nd, 2 * h + 1 - c, 2 * (1 - h) + c, 2 * (1 - h) + 1 - c]
    targets = [nodes[0], nodes[2]]
    flat = lambda f: [f(m, j) for m in range(NODES) for j in range(NODES)]
    q_u = flat(lambda m, j: time_step * diffusion * SCALE[m] * QUAD[m][j])
    q_r = flat(lambda m, j: time_step * SCALE[m] * QUAD[m][j])
    cu = [[pick(q_u, t * NODES + n) for n in nodes] for t in targets]
    cr = [[pick(q_r, t * NODES + n) for n in nodes] for t in targets]
    cs = [pick(SCALE, t) for t in targets]
    beta = [pick(BETA, t) for t in targets]
    wt = [pick([time_step * w for w in WEIGHTS], n) for n in nodes]
    wx = [wt[0], wt[2]]

    def nonlinear(x):
        return x * (LINEAR - reaction * (x * x))

    def point(i):
        xs = [XB[s, i] for s in range(4)]
        ns = [nonlinear(x) for x in xs]
        for t in range(2):
            UB[t, i] = (cu[t][0] * xs[0] + cu[t][1] * xs[1]) + (cu[t][2] * xs[2] + cu[t][3] * xs[3])
            RB[t, i] = ((cr[t][0] * ns[0] + cr[t][1] * ns[1]) + (cr[t][2] * ns[2] + cr[t][3] * ns[3])) - cs[t] * xs[2 * t]

    def end_old(k):
        p = k + c * (7 - 2 * k)
        i = p + H
        mix = lambda i: (wt[0] * XB[0, i] + wt[1] * XB[1, i]) + (wt[2] * XB[2, i] + wt[3] * XB[3, i])
        u = mix(i)
        total = mix(i - 1) + mix(i + 1) + flat_ring(u)
        rest = BG[p + 3]
        for s in range(4):
            rest = rest + wt[s] * nonlinear(XB[s, i])
        EO[k] = rest + diffusion * total

    loads[0].wait()

    @pl.when(tm == 0)
    def _():
        begin_load.wait()

    f2.wait_recv()
    for k in range(5):
        if k < 4:
            pair = (k, 7 - k)
            for p in pair:
                f1[p].wait_recv()
                across[p].start()
                along[p].start()
            for p in pair:
                f3[p].wait_recv()
                own_rim[p].start()
            for p in pair:
                across[p].wait_recv()
                point(H + p)
        if k > 0:
            pair = (k - 1, 8 - k)
            for p in pair:
                along[p].wait_recv()
                far_rim[p].start()

            if k == 1:
                @pl.when(tm == 0)
                def _():
                    b0.wait_recv()
                    b1.start()
            for p in pair:
                own_rim[p].wait_recv()
                far_rim[p].wait_recv()
                point(rim(p))

            @pl.when(tm == 0)
            def _():
                end_old(k - 1)
                for m in eo[k - 1]:
                    m.start()

    @pl.when(tm == 1)
    def _():
        for k in range(4):
            for m in eo[k]:
                m.wait_recv()
            for m in eb[k]:
                m.start()
        for k in range(3):
            eb[k][1].wait_recv()
        b1.start()
        for k in range(4):
            eb[k][0].wait_recv()

    b1.wait_recv()

    def first(j, carry):
        for t in range(2):
            u = UB[t, j + 1]
            DA[t, j] = (RB[t, j + 1] + cs[t] * BG[j]) + ((UB[t, j] + UB[t, j + 2]) + flat_ring(u))
        return carry

    lax.fori_loop(0, 14, first, 0)

    def stage(src, dst):
        def body(j, carry):
            for t in range(2):
                d = src[t, j]
                dst[t, j] = DA[t, j] + beta[t] * ((src[t, j - 1] + src[t, j + 1]) + flat_ring(d))
            return carry
        return body

    DC = UB
    lax.fori_loop(1, 13, stage(DA, DB), 0)
    lax.fori_loop(2, 12, stage(DB, DC), 0)

    def last(j, carry):
        total = None
        for t in range(2):
            d = DC[t, j]
            x = XB[2 * t, j + 1] + (DA[t, j] + beta[t] * ((DC[t, j - 1] + DC[t, j + 1]) + flat_ring(d)))
            DB[t, j] = x
            total = wx[t] * x if total is None else total + wx[t] * x
        UX[j - 2] = total
        return carry

    edge = [message(UX.at[1], UX.at[9], ZM), message(UX.at[8], UX.at[0], ZP)]
    for j in (3, 10):
        last(j, 0)
    for m in edge:
        m.start()
    lax.fori_loop(4, 10, last, 0)
    out_new = pltpu.make_async_copy(DB.at[0, pl.ds(3, 8)], new_ref.at[0, 0], local.at[2])
    out_new.start()

    def force(p):
        u = UX[p + 1]
        VB[p] = (wx[0] * nonlinear(DB[0, p + 3]) + wx[1] * nonlinear(DB[1, p + 3])) + diffusion * (
            (UX[p] + UX[p + 2]) + flat_ring(u))

    swap = [message(VB.at[pl.ds(1, 6)], VR.at[pl.ds(1, 6)], SIB),
            message(VB.at[0], VR.at[0], SIB), message(VB.at[7], VR.at[7], SIB)]

    def inner(p, carry):
        force(p)
        return carry

    lax.fori_loop(1, 7, inner, 0)
    swap[0].start()
    for m in edge:
        m.wait_recv()
    force(0)
    force(7)
    swap[1].start()
    swap[2].start()

    def finish(p, carry):
        VB[p + 8] = BG[p + 3] + (VB[p] + VR[p])
        return carry

    for m in swap:
        m.wait_recv()
    lax.fori_loop(0, 8, finish, 0)
    out_end = pltpu.make_async_copy(VB.at[pl.ds(8, 8)], end_ref.at[0], local.at[3])
    out_end.start()
    for m in list(f1.values()) + [f2] + list(f3.values()) + list(across.values()) + list(along.values()) \
            + list(own_rim.values()) + list(far_rim.values()) + [b1] + edge + swap:
        m.wait_send()

    @pl.when(tm == 0)
    def _():
        b0.wait_send()
        for k in range(4):
            for m in eo[k]:
                m.wait_send()

    @pl.when(tm == 1)
    def _():
        for k in range(4):
            for m in eb[k]:
                m.wait_send()

    out_new.wait()
    out_end.wait()
    assert count[0] <= NMSG


def on_device(spaces, start_old, nodes_old):
    import functools
    plane = (128, 256)
    V = lambda *lead: pltpu.VMEM(lead + plane, jnp.float32)
    new, end = pl.pallas_call(
        functools.partial(kernel, spaces),
        out_shape=(jax.ShapeDtypeStruct(nodes_old.shape, jnp.float32),
                   jax.ShapeDtypeStruct(start_old.shape, jnp.float32)),
        in_specs=[pl.BlockSpec(memory_space=pl.ANY)] * 2,
        out_specs=(pl.BlockSpec(memory_space=pl.ANY),) * 2,
        scratch_shapes=[V(4, 16), V(2, 16), V(2, 16), V(14), V(2, 14), V(2, 14), V(4), V(10), V(16), V(8),
                        pltpu.SemaphoreType.DMA((NMSG,)), pltpu.SemaphoreType.DMA((NMSG,)),
                        pltpu.SemaphoreType.DMA((4,))],
        compiler_params=pltpu.CompilerParams(collective_id=0, has_side_effects=True),
    )(start_old, nodes_old)
    return new, end


def solution(mesh):
    import functools
    return jax.shard_map(
        functools.partial(on_device, mesh.shape["space"]),
        mesh=mesh,
        in_specs=(P("tm", "space", None, None), P("tm", "node", "space", None, None)),
        out_specs=(P("tm", "node", "space", None, None), P("tm", "space", None, None)),
        check_vma=False,
    )
```
